1024 devices in a mesh: tower: 32 (over x_lo, y, core), intra: 32 (over z, x_hi).
Axes of the slice: x: 4 (x_hi: 2, x_lo: 2; x = x_hi * 2 + x_lo), y: 8, z: 16, core: 2. Of those that a mesh axis runs over, the one named last changes fastest.
Arguments:
- ids: int32 [256, 2, 8192], P('tower', None, 'intra'), may hold values from 0 to 511
- arrival: int32 [256, 8192], P('tower', 'intra'), may hold values from 0 to 255, as said below
- tables: bfloat16 [256, 16384, 128], P('tower', 'intra'), may hold values from -6 to 6
- cross_weight: bfloat16 [32, 2, 1024, 1024], P('tower'), may hold values from -0.1875 to 0.1875
- cross_bias: float32 [32, 2, 1024], P('tower'), may hold values from -4 to 4
- compress_weight: bfloat16 [32, 1024, 128], P('tower'), may hold values from -0.1875 to 0.1875
- over_weight: bfloat16 [4096, 512], replicated, may hold values from -0.09375 to 0.09375
- over_bias: float32 [512], replicated, may hold values from -4 to 4
- cotangent: bfloat16 [32, 32, 8, 512], P('intra', 'tower'), may hold values from -6 to 6
Outputs:
- over_out: bfloat16 [32, 32, 8, 512], P('intra', 'tower')
- pooled_grad: bfloat16 [256, 8192, 128], P('tower', 'intra')
The draws below stay inside these ranges and needn't reach their ends.
Inputs may be any that keep to these rules, and one draw needn't show every extreme that they name: `ids`: row numbers within the table shard that holds the slot. `arrival`: for each feature, every aligned block of 256 positions holds each number 0 to 255 once.
All inputs are finite; a program needn't handle non-finite values.
Results may differ from the reference program's by a relative error of at most 0.018.
Values may be sent and summed in bfloat16 or wider, within the bound.
A program may use at most 32 MiB of HBM per device.

```python
import jax
import jax.numpy as jnp
from jax import lax

F = 8
E = 128
ROWS = 16384
BAG = 2
LAYERS = 2
C = 128
OUT = 512
SAMP_DEV = 256
D = 1024
SAMPLES = 8192
BLOCK = 8
OVER_IN = 4096
TF = 256
ROWS_DEV = 512
SLOT_PEER = 8
N_TOWER = 32
N_INTRA = 32


def draw_arrival(key, part):
    keys = jax.random.split(jax.random.fold_in(key, 17), TF * N_INTRA)
    perms = jax.vmap(lambda one: jax.random.permutation(one, SAMP_DEV))(keys)
    return perms.reshape(TF, SAMPLES).astype(jnp.int32)


def plant(values, stream_key, least, high):
    shape = values.shape
    spot = [jax.random.randint(jax.random.fold_in(stream_key, axis), (), 0, shape[axis]) for axis in range(len(shape))]
    values = values.at[tuple(spot)].set(least)
    longest = shape.index(max(shape))
    spot[longest] = (spot[longest] + 1) % shape[longest]
    return values.at[tuple(spot)].set(high)


def shard_levels(rng, extent, pieces, least, top_value):
    level = 1.0
    for axis_at, blocks in pieces:
        steps = jax.random.uniform(jax.random.fold_in(jax.random.fold_in(rng, 6), axis_at), (blocks,), jnp.float32, least / len(pieces), top_value / len(pieces))
        level = level * jnp.repeat(jnp.exp(steps), extent[axis_at] // blocks).reshape((-1,) + (1,) * (len(extent) - 1 - axis_at))
    return level


def scatter_about(key, extent, scale, bound, cuts=(), kind=jnp.bfloat16):
    gain = shard_levels(key, extent, cuts, -0.22, 0.18) if cuts else 1.0
    array = jax.random.normal(key, extent, jnp.float32) * scale * gain
    return jnp.minimum(jnp.maximum(array, -bound), bound).astype(kind)


def setup_inputs(seed: int = 0) -> dict:
    streams_of = jax.random.split(jax.random.key(seed), 10)
    ids = plant(jax.random.randint(streams_of[0], (TF, BAG, SAMPLES), 0, ROWS_DEV), jax.random.fold_in(streams_of[0], 1), 0, ROWS_DEV - 1).astype(jnp.int32)
    arrival = draw_arrival(jax.random.fold_in(streams_of[9], 71), 0)
    tables = scatter_about(streams_of[2], (TF, ROWS, E), 0.7, 6.0, ((0, 32), (1, 32)))
    cross_weight = scatter_about(streams_of[3], (N_TOWER, LAYERS, D, D), D ** -0.5, 0.1875, ((0, 32),))
    cross_bias = scatter_about(streams_of[4], (N_TOWER, LAYERS, D), 0.5, 4.0, ((0, 32),), jnp.float32)
    compress_weight = scatter_about(streams_of[5], (N_TOWER, D, C), D ** -0.5, 0.1875, ((0, 32),))
    over_weight = scatter_about(streams_of[6], (OVER_IN, OUT), OVER_IN ** -0.5, 0.09375)
    over_bias = scatter_about(streams_of[7], (OUT,), 0.5, 4.0, (), jnp.float32)
    cotangent = scatter_about(streams_of[8], (N_INTRA, N_TOWER, BLOCK, OUT), 1.0, 6.0, ((0, 32), (1, 32)))
    return {"ids": ids, "arrival": arrival, "tables": tables, "cross_weight": cross_weight, "cross_bias": cross_bias, "compress_weight": compress_weight, "over_weight": over_weight, "over_bias": over_bias, "cotangent": cotangent}


def silu_slope(value):
    sig = jax.nn.sigmoid(value)
    return sig * (1.0 + value * (1.0 - sig))


def slot_targets(arrive):
    slot = jnp.arange(SAMPLES, dtype=jnp.int32)
    shard = slot // SAMP_DEV
    owner = (slot % SAMP_DEV) // SLOT_PEER
    within = slot % SLOT_PEER
    pos = owner * SAMP_DEV + shard * SLOT_PEER + within
    return owner[None, :] * SAMP_DEV + jnp.take(arrive, pos, axis=1)


def cross_forward(table, index, arrive, weight, bias):
    slot = jnp.arange(SAMPLES, dtype=jnp.int32)
    rows = (slot // SAMP_DEV)[None, None, :] * ROWS_DEV + index
    looked = jax.vmap(lambda tab, idx: jnp.take(tab, idx, axis=0))(table, rows)
    slot_vals = jnp.sum(looked, axis=1, dtype=jnp.float32).astype(jnp.bfloat16)
    dest = slot_targets(arrive)
    pooled = jax.vmap(lambda d, v: jnp.zeros((SAMPLES, E), jnp.bfloat16).at[d].set(v))(dest, slot_vals)
    first = jnp.transpose(pooled, (1, 0, 2)).reshape(SAMPLES, F * E)
    first_f = first.astype(jnp.float32)
    state = first
    zlist = []
    for layer in range(LAYERS):
        zval = jnp.dot(state, weight[layer], preferred_element_type=jnp.float32) + bias[layer][None, :]
        zlist.append(zval)
        state = (first_f * zval + state.astype(jnp.float32)).astype(jnp.bfloat16)
    return first_f, state, zlist, dest


def tower_front(inputs):
    table, index, arrive, weight, bias, squeeze = inputs
    first_f, state, zlist, dest = cross_forward(table, index, arrive, weight, bias)
    return jnp.dot(state, squeeze, preferred_element_type=jnp.float32).astype(jnp.bfloat16)


def tower_back(inputs):
    table, index, arrive, weight, bias, squeeze, dcomp = inputs
    first_f, state, zlist, dest = cross_forward(table, index, arrive, weight, bias)
    grad = lax.dot_general(dcomp, squeeze, (((1,), (1,)), ((), ())), preferred_element_type=jnp.float32)
    direct = jnp.zeros_like(grad)
    for layer in reversed(range(LAYERS)):
        upd = (grad * first_f).astype(jnp.bfloat16)
        direct = direct + grad * zlist[layer]
        grad = grad + lax.dot_general(upd, weight[layer], (((1,), (1,)), ((), ())), preferred_element_type=jnp.float32)
    final = (grad + direct).astype(jnp.bfloat16).reshape(SAMPLES, F, E)
    by_feature = jnp.transpose(final, (1, 0, 2))
    return jax.vmap(lambda d, v: jnp.take(v, d, axis=0))(dest, by_feature)


def reference(ids, arrival, tables, cross_weight, cross_bias, compress_weight, over_weight, over_bias, cotangent):
    table_t = tables.reshape(N_TOWER, F, ROWS, E)
    index_t = ids.reshape(N_TOWER, F, BAG, SAMPLES)
    arrive_t = arrival.reshape(N_TOWER, F, SAMPLES)
    comps = lax.map(tower_front, (table_t, index_t, arrive_t, cross_weight, cross_bias, compress_weight))
    joined = jnp.transpose(comps, (1, 0, 2)).reshape(SAMPLES, N_TOWER * C)
    pre = jnp.dot(joined, over_weight, preferred_element_type=jnp.float32) + over_bias
    over_out = jax.nn.silu(pre).astype(jnp.bfloat16).reshape(N_INTRA, N_TOWER, BLOCK, OUT)
    incoming = cotangent.reshape(SAMPLES, OUT).astype(jnp.float32)
    dz = (incoming * silu_slope(pre)).astype(jnp.bfloat16)
    d_in = lax.dot_general(dz, over_weight, (((1,), (1,)), ((), ())), preferred_element_type=jnp.float32).astype(jnp.bfloat16)
    dcomps = jnp.transpose(d_in.reshape(SAMPLES, N_TOWER, C), (1, 0, 2))
    grads = lax.map(tower_back, (table_t, index_t, arrive_t, cross_weight, cross_bias, compress_weight, dcomps))
    return over_out, grads.reshape(N_TOWER * F, SAMPLES, E)
```

```python
import functools

import jax
import jax.numpy as jnp
from jax import lax
from jax.experimental import pallas as pl
from jax.experimental.pallas import tpu as pltpu
from jax.sharding import PartitionSpec as P

MESH = pl.DeviceIdType.MESH
F32 = jnp.float32
BF16 = jnp.bfloat16
NT_DIMS = (((1,), (1,)), ((), ()))


def dot(a, b):
    return jnp.dot(a, b, preferred_element_type=F32)


def dot_t(a, b):
    return lax.dot_general(a, b, NT_DIMS, preferred_element_type=F32)


def kernel(
    ni,
    nt,
    ids_hbm,
    arr_hbm,
    tab_hbm,
    cw_hbm,
    cb_hbm,
    sq_hbm,
    ow_hbm,
    ob_hbm,
    ct_hbm,
    out_ref,
    grad_ref,
    ids_ref,
    arr_ref,
    tab_ref,
    cw_ref,
    cb_ref,
    sq_ref,
    ow_ref,
    ob_ref,
    ct_ref,
    send1,
    recv1,
    csend,
    joined,
    dsend,
    dcomp,
    send2,
    perm,
    perm_t,
    first,
    state1,
    state2,
    zbuf,
    gbuf,
    direct,
    upd,
    final,
    in_sem,
    own_sem,
    send_sem,
    recv_sem,
):
    feats, rows, embed = tab_ref.shape
    samp = arr_ref.shape[1]
    width = cw_ref.shape[2]
    block = samp // ni
    half = ni // 2
    tile = min(256, width)
    tiles = width // tile
    me_i = lax.axis_index("intra")
    me_t = lax.axis_index("tower")

    barrier = pltpu.get_barrier_semaphore()

    def greet_i(step, carry):
        peer = lax.rem(me_i + step, ni)
        pl.semaphore_signal(barrier, inc=1, device_id={"intra": peer}, device_id_type=MESH)
        return carry

    def greet_t(step, carry):
        peer = lax.rem(me_t + step, nt)
        pl.semaphore_signal(barrier, inc=1, device_id={"tower": peer}, device_id_type=MESH)
        return carry

    lax.fori_loop(1, ni, greet_i, 0)
    lax.fori_loop(1, nt, greet_t, 0)

    loads = [
        pltpu.make_async_copy(src, dst, in_sem.at[at])
        for at, (src, dst) in enumerate(
            (
                (ids_hbm, ids_ref),
                (arr_hbm, arr_ref),
                (tab_hbm, tab_ref),
                (cw_hbm.at[0], cw_ref),
                (cb_hbm.at[0], cb_ref),
                (sq_hbm.at[0], sq_ref),
                (ow_hbm, ow_ref),
                (ob_hbm, ob_ref),
                (ct_hbm.at[0, 0], ct_ref),
            )
        )
    ]
    for load in loads:
        load.start()
    loads[0].wait()
    loads[1].wait()

    ids = ids_ref[...].reshape(feats * 2, samp)
    arr = arr_ref[...]
    pad = jnp.zeros((128 - 3 * feats, samp), jnp.int32)
    columns = jnp.concatenate([ids, arr, pad], axis=0).T

    loads[2].wait()
    row_id = lax.broadcasted_iota(jnp.int32, (samp, rows), 1)
    for f in range(feats):
        hot = jnp.where(columns[:, 2 * f : 2 * f + 1] == row_id, 1.0, 0.0)
        hot = hot + jnp.where(columns[:, 2 * f + 1 : 2 * f + 2] == row_id, 1.0, 0.0)
        pooled = dot(hot.astype(BF16), tab_ref[f])
        send1[:, f] = pooled.reshape(ni, block, embed).astype(BF16)

    pl.semaphore_wait(barrier, ni + nt - 2)

    def peer_of(step):
        k = step // 2
        near = half // 2 - (k + 1) // 2
        far = half // 2 + k // 2
        dz = jnp.where(lax.rem(k, 2) == 1, near, far)
        z = lax.rem(me_i // 2 + dz, half)
        xh = lax.rem(lax.rem(me_i, 2) + 1 - lax.rem(step, 2), 2)
        return z * 2 + xh

    def exchange(src, dst, send, recv, axis, count, me, dst_at):
        def start(step, carry):
            if axis == "intra":
                peer = peer_of(step)
            else:
                peer = lax.rem(me + step + 1, count)
            pltpu.make_async_remote_copy(
                src_ref=src(peer),
                dst_ref=dst(me),
                send_sem=send,
                recv_sem=recv,
                device_id={axis: peer},
                device_id_type=MESH,
            ).start()
            return carry

        lax.fori_loop(0, count - 1, start, 0)
        own = pltpu.make_async_copy(src(me), dst(me), own_sem.at[dst_at])
        own.start()
        return own

    own1 = exchange(
        lambda p: send1.at[p], lambda p: recv1.at[p], send_sem.at[0], recv_sem.at[0], "intra", ni, me_i, 0
    )

    s_row = lax.broadcasted_iota(jnp.int32, (samp, samp), 0)
    s_col = lax.broadcasted_iota(jnp.int32, (samp, samp), 1)
    for f in range(feats):
        perm[f] = jnp.where(arr[f : f + 1, :] == s_row, 1.0, 0.0).astype(BF16)
        at = 2 * feats + f
        perm_t[f] = jnp.where(columns[:, at : at + 1] == s_col, 1.0, 0.0).astype(BF16)
    for load in loads[3:]:
        load.wait()

    def all_but_one(ref, sem, count):
        pltpu.make_async_copy(ref.at[pl.ds(0, count - 1)], ref.at[pl.ds(0, count - 1)], sem).wait()

    own1.wait()
    all_but_one(recv1, recv_sem.at[0], ni)

    for f in range(feats):
        got = recv1[:, f].astype(F32).reshape(samp, embed).astype(BF16)
        first[:, f * embed : (f + 1) * embed] = dot(perm[f], got).astype(BF16)

    def forward(layer, src, dst):
        def step(n, carry):
            cols = pl.ds(pl.multiple_of(n * tile, tile), tile)
            zval = dot(src[...], cw_ref[layer, :, cols]) + cb_ref[pl.ds(layer, 1), cols]
            zbuf[layer, :, cols] = zval
            dst[:, cols] = (first[:, cols].astype(F32) * zval + src[:, cols].astype(F32)).astype(BF16)
            return carry

        lax.fori_loop(0, tiles, step, 0)

    forward(0, first, state1)
    forward(1, state1, state2)
    csend[...] = dot(state2[...], sq_ref[...]).reshape(nt, samp // nt, -1).astype(BF16)

    own2 = exchange(
        lambda p: csend.at[p], lambda p: joined.at[p], send_sem.at[1], recv_sem.at[1], "tower", nt, me_t, 1
    )
    own2.wait()
    all_but_one(joined, recv_sem.at[1], nt)

    comp = joined.shape[2]
    whole = jnp.concatenate([joined[t] for t in range(nt)], axis=1)
    pre = dot(whole, ow_ref[...]) + ob_ref[...]
    sig = jax.nn.sigmoid(pre)
    out_ref[0, 0] = (pre * sig).astype(BF16)
    dz = (ct_ref[...].astype(F32) * (sig * (1.0 + pre * (1.0 - sig)))).astype(BF16)
    d_in = dot_t(dz, ow_ref[...]).astype(BF16)
    for t in range(nt):
        dsend[t] = d_in[:, t * comp : (t + 1) * comp]

    own3 = exchange(
        lambda p: dsend.at[p], lambda p: dcomp.at[p], send_sem.at[2], recv_sem.at[2], "tower", nt, me_t, 2
    )
    own3.wait()
    all_but_one(dcomp, recv_sem.at[2], nt)

    dc = dcomp[...].astype(F32).reshape(samp, comp).astype(BF16)

    def back_top(n, carry):
        cols = pl.ds(pl.multiple_of(n * tile, tile), tile)
        grad = dot_t(dc, sq_ref[cols, :])
        gbuf[:, cols] = grad
        direct[:, cols] = grad * zbuf[1, :, cols]
        upd[1, :, cols] = (grad * first[:, cols].astype(F32)).astype(BF16)
        return carry

    def back_one(n, carry):
        cols = pl.ds(pl.multiple_of(n * tile, tile), tile)
        grad = gbuf[:, cols] + dot_t(upd[1], cw_ref[1, cols, :])
        gbuf[:, cols] = grad
        direct[:, cols] += grad * zbuf[0, :, cols]
        upd[0, :, cols] = (grad * first[:, cols].astype(F32)).astype(BF16)
        return carry

    def back_zero(n, carry):
        cols = pl.ds(pl.multiple_of(n * tile, tile), tile)
        grad = gbuf[:, cols] + dot_t(upd[0], cw_ref[0, cols, :])
        final[:, cols] = (grad + direct[:, cols]).astype(BF16)
        return carry

    lax.fori_loop(0, tiles, back_top, 0)
    lax.fori_loop(0, tiles, back_one, 0)
    lax.fori_loop(0, tiles, back_zero, 0)
    for f in range(feats):
        leaving = dot(perm_t[f], final[:, f * embed : (f + 1) * embed])
        send2[:, f] = leaving.reshape(ni, block, embed).astype(BF16)

    own4 = exchange(
        lambda p: send2.at[p], lambda p: grad_ref.at[:, p], send_sem.at[3], recv_sem.at[3], "intra", ni, me_i, 3
    )
    own4.wait()
    pltpu.make_async_copy(
        grad_ref.at[:, pl.ds(0, ni - 1)], grad_ref.at[:, pl.ds(0, ni - 1)], recv_sem.at[3]
    ).wait()
    all_but_one(send1, send_sem.at[0], ni)
    all_but_one(csend, send_sem.at[1], nt)
    all_but_one(dsend, send_sem.at[2], nt)
    all_but_one(send2, send_sem.at[3], ni)


def local(ids, arrival, tables, cross_weight, cross_bias, squeeze, over_weight, over_bias, cotangent, ni, nt):
    feats, rows, embed = tables.shape
    samp = arrival.shape[1]
    width = cross_weight.shape[2]
    comp = squeeze.shape[2]
    wide = over_weight.shape[1]
    rblock = cotangent.shape[2]
    block = samp // ni
    any_spec = pl.BlockSpec(memory_space=pl.ANY)
    vmem_spec = pl.BlockSpec(memory_space=pltpu.VMEM)
    over_out, grad = pl.pallas_call(
        functools.partial(kernel, ni, nt),
        out_shape=(
            jax.ShapeDtypeStruct(cotangent.shape, BF16),
            jax.ShapeDtypeStruct((feats, ni, block, embed), BF16),
        ),
        in_specs=[any_spec] * 9,
        out_specs=(vmem_spec, vmem_spec),
        scratch_shapes=[
            pltpu.VMEM((feats, 2, samp), jnp.int32),
            pltpu.VMEM((feats, samp), jnp.int32),
            pltpu.VMEM((feats, rows, embed), BF16),
            pltpu.VMEM((2, width, width), BF16),
            pltpu.VMEM((2, width), F32),
            pltpu.VMEM((width, comp), BF16),
            pltpu.VMEM((nt * comp, wide), BF16),
            pltpu.VMEM((1, wide), F32),
            pltpu.VMEM((rblock, wide), BF16),
            pltpu.VMEM((ni, feats, block, embed), BF16),
            pltpu.VMEM((ni, feats, block, embed), BF16),
            pltpu.VMEM((nt, rblock, comp), BF16),
            pltpu.VMEM((nt, rblock, comp), BF16),
            pltpu.VMEM((nt, rblock, comp), BF16),
            pltpu.VMEM((nt, rblock, comp), BF16),
            pltpu.VMEM((ni, feats, block, embed), BF16),
            pltpu.VMEM((feats, samp, samp), BF16),
            pltpu.VMEM((feats, samp, samp), BF16),
            pltpu.VMEM((samp, width), BF16),
            pltpu.VMEM((samp, width), BF16),
            pltpu.VMEM((samp, width), BF16),
            pltpu.VMEM((2, samp, width), F32),
            pltpu.VMEM((samp, width), F32),
            pltpu.VMEM((samp, width), F32),
            pltpu.VMEM((2, samp, width), BF16),
            pltpu.VMEM((samp, width), BF16),
            pltpu.SemaphoreType.DMA((9,)),
            pltpu.SemaphoreType.DMA((4,)),
            pltpu.SemaphoreType.DMA((4,)),
            pltpu.SemaphoreType.DMA((4,)),
        ],
        compiler_params=pltpu.CompilerParams(
            collective_id=0, has_side_effects=True, vmem_limit_bytes=60 * 1024 * 1024
        ),
    )(ids, arrival, tables, cross_weight, cross_bias, squeeze, over_weight, over_bias[None, :], cotangent)
    return over_out, grad.reshape(feats, samp, embed)


def solution(mesh):
    in_specs = (
        P("tower", None, "intra"),
        P("tower", "intra"),
        P("tower", "intra", None),
        P("tower", None, None, None),
        P("tower", None, None),
        P("tower", None, None),
        P(),
        P(),
        P("intra", "tower", None, None),
    )
    out_specs = (P("intra", "tower", None, None), P("tower", "intra", None))
    body = functools.partial(local, ni=mesh.shape["intra"], nt=mesh.shape["tower"])
    return jax.shard_map(body, mesh=mesh, in_specs=in_specs, out_specs=out_specs, check_vma=False)
```

```python
import functools

import jax
import jax.numpy as jnp
from jax import lax
from jax.experimental import pallas as pl
from jax.experimental.pallas import tpu as pltpu
from jax.sharding import PartitionSpec as P

MESH = pl.DeviceIdType.MESH
F32 = jnp.float32
BF16 = jnp.bfloat16
NT_DIMS = (((1,), (1,)), ((), ()))


def dot(a, b):
    return jnp.dot(a, b, preferred_element_type=F32)


def dot_t(a, b):
    return lax.dot_general(a, b, NT_DIMS, preferred_element_type=F32)


def kernel(
    ni,
    nt,
    groups,
    ids_hbm,
    arr_hbm,
    tab_hbm,
    cw_hbm,
    cb_hbm,
    sq_hbm,
    ow_hbm,
    ob_hbm,
    ct_hbm,
    out_ref,
    grad_ref,
    ids_ref,
    arr_ref,
    tab_ref,
    cw_ref,
    cb_ref,
    sq_ref,
    ow_ref,
    ob_ref,
    ct_ref,
    send1,
    recv1,
    csend,
    joined,
    dsend,
    dcomp,
    send2,
    perm,
    perm_t,
    first,
    state1,
    state2,
    zbuf,
    gbuf,
    direct,
    upd,
    final,
    in_sem,
    own_sem,
    send_sem,
    recv_sem,
):
    feats, rows, embed = tab_ref.shape
    samp = arr_ref.shape[1]
    width = cw_ref.shape[2]
    block = samp // ni
    half = ni // 2
    tile = min(256, width)
    tiles = width // tile
    me_i = lax.axis_index("intra")
    me_t = lax.axis_index("tower")

    barrier = pltpu.get_barrier_semaphore()

    def peer_of(step, sets):
        each = half // sets
        k = lax.rem(step // 2, each)
        near = -((k + 1) // 2)
        shift = jnp.where(lax.rem(k, 2) == 1, near, k // 2) + each // 2
        base = lax.rem((step // 2) // each + half - me_i // 2, sets)
        z = lax.rem(me_i // 2 + base + sets * shift, half)
        xh = lax.rem(lax.rem(me_i, 2) + 1 - lax.rem(step, 2), 2)
        return z * 2 + xh

    def greet_i(step, carry):
        peer = peer_of(step, 1)
        pl.semaphore_signal(barrier, inc=1, device_id={"intra": peer}, device_id_type=MESH)
        return carry

    def greet_t(step, carry):
        peer = lax.rem(me_t + step, nt)
        pl.semaphore_signal(barrier, inc=1, device_id={"tower": peer}, device_id_type=MESH)
        return carry

    lax.fori_loop(0, ni - 1, greet_i, 0)
    lax.fori_loop(1, nt, greet_t, 0)

    loads = [
        pltpu.make_async_copy(src, dst, in_sem.at[at])
        for at, (src, dst) in enumerate(
            (
                (ids_hbm, ids_ref),
                (arr_hbm, arr_ref),
                (tab_hbm, tab_ref),
                (cw_hbm.at[0], cw_ref),
                (cb_hbm.at[0], cb_ref),
                (sq_hbm.at[0], sq_ref),
                (ow_hbm, ow_ref),
                (ob_hbm, ob_ref),
                (ct_hbm.at[0, 0], ct_ref),
            )
        )
    ]
    for load in loads:
        load.start()
    loads[0].wait()
    loads[1].wait()

    ids = ids_ref[...].reshape(feats * 2, samp)
    arr = arr_ref[...]
    pad = jnp.zeros((128 - 3 * feats, samp), jnp.int32)
    columns = jnp.concatenate([ids, arr, pad], axis=0).T

    loads[2].wait()
    row_id = lax.broadcasted_iota(jnp.int32, (samp, rows), 1)
    for f in range(feats):
        hot = jnp.where(columns[:, 2 * f : 2 * f + 1] == row_id, 1.0, 0.0)
        hot = hot + jnp.where(columns[:, 2 * f + 1 : 2 * f + 2] == row_id, 1.0, 0.0)
        pooled = dot(hot.astype(BF16), tab_ref[f])
        send1[:, f] = pooled.reshape(ni, block, embed).astype(BF16)

    pl.semaphore_wait(barrier, ni + nt - 2)

    def exchange_i(src, dst, at, sets):
        own = pltpu.make_async_copy(src(me_i), dst(me_i), own_sem.at[at])
        own.start()

        def start(step, carry):
            peer = peer_of(step, sets)

            @pl.when(peer != me_i)
            def _():
                pltpu.make_async_remote_copy(
                    src_ref=src(peer),
                    dst_ref=dst(me_i),
                    send_sem=send_sem.at[at],
                    recv_sem=recv_sem.at[at],
                    device_id={"intra": peer},
                    device_id_type=MESH,
                ).start()

            return carry

        lax.fori_loop(0, ni, start, 0)
        return own

    def exchange_t(src, dst, at):
        own = pltpu.make_async_copy(src(me_t), dst(me_t), own_sem.at[at])
        own.start()

        def start(step, carry):
            peer = lax.rem(me_t + step, nt)
            pltpu.make_async_remote_copy(
                src_ref=src(peer),
                dst_ref=dst(me_t),
                send_sem=send_sem.at[at],
                recv_sem=recv_sem.at[at],
                device_id={"tower": peer},
                device_id_type=MESH,
            ).start()
            return carry

        lax.fori_loop(1, nt, start, 0)
        return own

    own1 = exchange_i(lambda p: send1.at[p], lambda p: recv1.at[p], 0, groups)

    s_row = lax.broadcasted_iota(jnp.int32, (samp, samp), 0)
    s_col = lax.broadcasted_iota(jnp.int32, (samp, samp), 1)
    for f in range(feats):
        perm[f] = jnp.where(arr[f : f + 1, :] == s_row, 1.0, 0.0).astype(BF16)
        at = 2 * feats + f
        perm_t[f] = jnp.where(columns[:, at : at + 1] == s_col, 1.0, 0.0).astype(BF16)
    for load in loads[3:]:
        load.wait()

    def all_but_one(ref, sem, count):
        pltpu.make_async_copy(ref.at[pl.ds(0, count - 1)], ref.at[pl.ds(0, count - 1)], sem).wait()

    own1.wait()
    all_but_one(recv1, recv_sem.at[0], ni)

    for f in range(feats):
        got = recv1[:, f].astype(F32).reshape(samp, embed).astype(BF16)
        first[:, f * embed : (f + 1) * embed] = dot(perm[f], got).astype(BF16)

    def forward(layer, src, dst):
        for n in range(tiles):
            cols = slice(n * tile, (n + 1) * tile)
            zval = dot(src[...], cw_ref[layer, :, cols]) + cb_ref[layer : layer + 1, cols]
            zbuf[layer, :, cols] = zval
            dst[:, cols] = (first[:, cols].astype(F32) * zval + src[:, cols].astype(F32)).astype(BF16)

    forward(0, first, state1)
    forward(1, state1, state2)
    csend[...] = dot(state2[...], sq_ref[...]).reshape(nt, samp // nt, -1).astype(BF16)

    own2 = exchange_t(lambda p: csend.at[p], lambda p: joined.at[p], 1)
    own2.wait()
    all_but_one(joined, recv_sem.at[1], nt)

    comp = joined.shape[2]
    whole = jnp.concatenate([joined[t] for t in range(nt)], axis=1)
    pre = dot(whole, ow_ref[...]) + ob_ref[...]
    sig = jax.nn.sigmoid(pre)
    out_ref[0, 0] = (pre * sig).astype(BF16)
    dz = (ct_ref[...].astype(F32) * (sig * (1.0 + pre * (1.0 - sig)))).astype(BF16)
    d_in = dot_t(dz, ow_ref[...]).astype(BF16)
    for t in range(nt):
        dsend[t] = d_in[:, t * comp : (t + 1) * comp]

    own3 = exchange_t(lambda p: dsend.at[p], lambda p: dcomp.at[p], 2)
    own3.wait()
    all_but_one(dcomp, recv_sem.at[2], nt)

    dc = dcomp[...].astype(F32).reshape(samp, comp).astype(BF16)

    def back_top(n):
        cols = slice(n * tile, (n + 1) * tile)
        grad = dot_t(dc, sq_ref[cols, :])
        gbuf[:, cols] = grad
        direct[:, cols] = grad * zbuf[1, :, cols]
        upd[1, :, cols] = (grad * first[:, cols].astype(F32)).astype(BF16)

    def back_one(n):
        cols = slice(n * tile, (n + 1) * tile)
        grad = gbuf[:, cols] + dot_t(upd[1], cw_ref[1, cols, :])
        gbuf[:, cols] = grad
        direct[:, cols] += grad * zbuf[0, :, cols]
        upd[0, :, cols] = (grad * first[:, cols].astype(F32)).astype(BF16)

    def back_zero(n):
        cols = slice(n * tile, (n + 1) * tile)
        grad = gbuf[:, cols] + dot_t(upd[0], cw_ref[0, cols, :])
        final[:, cols] = (grad + direct[:, cols]).astype(BF16)

    for n in range(tiles):
        back_top(n)
    for n in range(tiles):
        back_one(n)
    for n in range(tiles):
        back_zero(n)
    for f in range(feats):
        leaving = dot(perm_t[f], final[:, f * embed : (f + 1) * embed])
        send2[:, f] = leaving.reshape(ni, block, embed).astype(BF16)

    own4 = exchange_i(lambda p: send2.at[p], lambda p: grad_ref.at[:, p], 3, 1)
    own4.wait()
    pltpu.make_async_copy(
        grad_ref.at[:, pl.ds(0, ni - 1)], grad_ref.at[:, pl.ds(0, ni - 1)], recv_sem.at[3]
    ).wait()
    all_but_one(send1, send_sem.at[0], ni)
    all_but_one(csend, send_sem.at[1], nt)
    all_but_one(dsend, send_sem.at[2], nt)
    all_but_one(send2, send_sem.at[3], ni)


def local(ids, arrival, tables, cross_weight, cross_bias, squeeze, over_weight, over_bias, cotangent, ni, nt, groups=4, cid=0, name=None, vmem=32):
    feats, rows, embed = tables.shape
    samp = arrival.shape[1]
    width = cross_weight.shape[2]
    comp = squeeze.shape[2]
    wide = over_weight.shape[1]
    rblock = cotangent.shape[2]
    block = samp // ni
    any_spec = pl.BlockSpec(memory_space=pltpu.HBM)
    vmem_spec = pl.BlockSpec(memory_space=pltpu.VMEM)
    over_out, grad = pl.pallas_call(
        functools.partial(kernel, ni, nt, groups),
        out_shape=(
            jax.ShapeDtypeStruct(cotangent.shape, BF16),
            jax.ShapeDtypeStruct((feats, ni, block, embed), BF16),
        ),
        in_specs=[any_spec] * 9,
        name=name,
        out_specs=(vmem_spec, vmem_spec),
        scratch_shapes=[
            pltpu.VMEM((feats, 2, samp), jnp.int32),
            pltpu.VMEM((feats, samp), jnp.int32),
            pltpu.VMEM((feats, rows, embed), BF16),
            pltpu.VMEM((2, width, width), BF16),
            pltpu.VMEM((2, width), F32),
            pltpu.VMEM((width, comp), BF16),
            pltpu.VMEM((nt * comp, wide), BF16),
            pltpu.VMEM((1, wide), F32),
            pltpu.VMEM((rblock, wide), BF16),
            pltpu.VMEM((ni, feats, block, embed), BF16),
            pltpu.VMEM((ni, feats, block, embed), BF16),
            pltpu.VMEM((nt, rblock, comp), BF16),
            pltpu.VMEM((nt, rblock, comp), BF16),
            pltpu.VMEM((nt, rblock, comp), BF16),
            pltpu.VMEM((nt, rblock, comp), BF16),
            pltpu.VMEM((ni, feats, block, embed), BF16),
            pltpu.VMEM((feats, samp, samp), BF16),
            pltpu.VMEM((feats, samp, samp), BF16),
            pltpu.VMEM((samp, width), BF16),
            pltpu.VMEM((samp, width), BF16),
            pltpu.VMEM((samp, width), BF16),
            pltpu.VMEM((2, samp, width), F32),
            pltpu.VMEM((samp, width), F32),
            pltpu.VMEM((samp, width), F32),
            pltpu.VMEM((2, samp, width), BF16),
            pltpu.VMEM((samp, width), BF16),
            pltpu.SemaphoreType.DMA((9,)),
            pltpu.SemaphoreType.DMA((4,)),
            pltpu.SemaphoreType.DMA((4,)),
            pltpu.SemaphoreType.DMA((4,)),
        ],
        compiler_params=pltpu.CompilerParams(
            collective_id=cid, has_side_effects=True, vmem_limit_bytes=vmem * 1024 * 1024
        ),
    )(
        *(
            pltpu.with_memory_space_constraint(x, pltpu.HBM)
            for x in (
                ids,
                arrival,
                tables,
                cross_weight,
                cross_bias,
                squeeze,
                over_weight,
                over_bias[None, :],
                cotangent,
            )
        )
    )
    return over_out, grad.reshape(feats, samp, embed)


def solution(mesh):
    in_specs = (
        P("tower", None, "intra"),
        P("tower", "intra"),
        P("tower", "intra", None),
        P("tower", None, None, None),
        P("tower", None, None),
        P("tower", None, None),
        P(),
        P(),
        P("intra", "tower", None, None),
    )
    out_specs = (P("intra", "tower", None, None), P("tower", "intra", None))
    body = functools.partial(local, ni=mesh.shape["intra"], nt=mesh.shape["tower"])
    return jax.shard_map(body, mesh=mesh, in_specs=in_specs, out_specs=out_specs, check_vma=False)
```

```python
import functools

import jax
import jax.numpy as jnp
from jax import lax
from jax.experimental import pallas as pl
from jax.experimental.pallas import tpu as pltpu
from jax.sharding import PartitionSpec as P

MESH = pl.DeviceIdType.MESH
F32 = jnp.float32
BF16 = jnp.bfloat16
NT_DIMS = (((1,), (1,)), ((), ()))


def dot(a, b):
    return jnp.dot(a, b, preferred_element_type=F32)


def dot_t(a, b):
    return lax.dot_general(a, b, NT_DIMS, preferred_element_type=F32)


def kernel(
    ni,
    nt,
    groups,
    ids_hbm,
    arr_hbm,
    tab_hbm,
    cw_hbm,
    cb_hbm,
    sq_hbm,
    ow_hbm,
    ob_hbm,
    ct_hbm,
    out_ref,
    grad_ref,
    ids_ref,
    arr_ref,
    tab_ref,
    cw_ref,
    cb_ref,
    sq_ref,
    ow_ref,
    ob_ref,
    ct_ref,
    send1,
    recv1,
    csend,
    joined,
    dsend,
    dcomp,
    send2,
    perm,
    perm_t,
    first,
    state1,
    state2,
    zbuf,
    gbuf,
    direct,
    upd,
    final,
    in_sem,
    own_sem,
    send_sem,
    recv_sem,
    ring_sem,
    over_sem,
    mate_sem,
):
    feats, rows, embed = tab_ref.shape
    samp = arr_ref.shape[1]
    width = cw_ref.shape[2]
    block = samp // ni
    half = ni // 2
    tile = min(256, width)
    tiles = width // tile
    me_i = lax.axis_index("intra")
    me_t = lax.axis_index("tower")

    zed, side = me_i // 2, lax.rem(me_i, 2)
    ring = nt // 4
    low, why, core = me_t // (2 * ring), lax.rem(me_t // 2, ring), lax.rem(me_t, 2)
    cut = max(0, half // 4 - 1)

    def at_i(dz, flip):
        return lax.rem(zed + dz + half, half) * 2 + lax.rem(side + flip, 2)

    def at_t(dy, flip_low, flip_core):
        return (
            lax.rem(low + flip_low, 2) * (2 * ring)
            + lax.rem(why + dy + ring, ring) * 2
            + lax.rem(core + flip_core, 2)
        )

    def signal(sem, axis, peer):
        pl.semaphore_signal(sem, inc=1, device_id={axis: peer}, device_id_type=MESH)

    barrier = pltpu.get_barrier_semaphore()
    greet = [("intra", at_i(0, 1)), ("intra", at_i(1, 0)), ("intra", at_i(-1, 0))]
    greet += [("tower", at_t(0, 1, 0)), ("tower", at_t(0, 0, 1))]
    if ring > 1:
        greet += [("tower", at_t(1, 0, 0)), ("tower", at_t(-1, 0, 0))]
    for axis, peer in greet:
        signal(barrier, axis, peer)

    def peer_of(step, sets):
        each = half // sets
        k = lax.rem(step // 2, each)
        near = -((k + 1) // 2)
        shift = jnp.where(lax.rem(k, 2) == 1, near, k // 2) + each // 2
        base = lax.rem((step // 2) // each + half - me_i // 2, sets)
        z = lax.rem(me_i // 2 + base + sets * shift, half)
        xh = lax.rem(lax.rem(me_i, 2) + 1 - lax.rem(step, 2), 2)
        return z * 2 + xh

    loads = [
        pltpu.make_async_copy(src, dst, in_sem.at[at])
        for at, (src, dst) in enumerate(
            (
                (ids_hbm, ids_ref),
                (arr_hbm, arr_ref),
                (tab_hbm, tab_ref),
                (cw_hbm.at[0], cw_ref),
                (cb_hbm.at[0], cb_ref),
                (sq_hbm.at[0], sq_ref),
                (ow_hbm, ow_ref),
                (ob_hbm, ob_ref),
                (ct_hbm.at[0, 0], ct_ref),
            )
        )
    ]
    for load in loads:
        load.start()
    loads[0].wait()
    loads[1].wait()

    ids = ids_ref[...].reshape(feats * 2, samp)
    arr = arr_ref[...]
    pad = jnp.zeros((128 - 3 * feats, samp), jnp.int32)
    columns = jnp.concatenate([ids, arr, pad], axis=0).T

    loads[2].wait()
    row_id = lax.broadcasted_iota(jnp.int32, (samp, rows), 1)
    for f in range(feats):
        hot = jnp.where(columns[:, 2 * f : 2 * f + 1] == row_id, 1.0, 0.0)
        hot = hot + jnp.where(columns[:, 2 * f + 1 : 2 * f + 2] == row_id, 1.0, 0.0)
        pooled = dot(hot.astype(BF16), tab_ref[f])
        send1[:, f] = pooled.reshape(ni, block, embed).astype(BF16)

    pl.semaphore_wait(barrier, len(greet))

    def send(src, dst, at, axis, peer, me):
        pltpu.make_async_remote_copy(
            src_ref=src(peer),
            dst_ref=dst(me),
            send_sem=send_sem.at[at],
            recv_sem=recv_sem.at[at],
            device_id={axis: peer},
            device_id_type=MESH,
        ).start()

    def exchange_i(src, dst, at, sets, fresh):
        own = pltpu.make_async_copy(src(me_i), dst(me_i), own_sem.at[at])
        own.start()
        if fresh:
            for step in range(half // 2 + 1):
                if step:
                    signal(ring_sem.at[step - 1, 0], "intra", at_i(1, 0))
                    signal(ring_sem.at[step - 1, 1], "intra", at_i(-1, 0))
                    pl.semaphore_wait(ring_sem.at[step - 1, 0], 1)
                    pl.semaphore_wait(ring_sem.at[step - 1, 1], 1)
                for dist, flip in ((step + 1, 0), (step, 1)):
                    if dist <= cut:
                        send(src, dst, at, "intra", at_i(dist, flip), me_i)
                        if dist:
                            send(src, dst, at, "intra", at_i(-dist, flip), me_i)

        def start(step, carry):
            peer = peer_of(step, sets)
            gap = lax.rem(peer // 2 - zed + half, half)
            if fresh:
                wanted = jnp.logical_and(gap > cut, gap < half - cut)
            else:
                wanted = peer != me_i

            @pl.when(wanted)
            def _():
                send(src, dst, at, "intra", peer, me_i)

            return carry

        lax.fori_loop(0, ni, start, 0)
        return own

    def exchange_t(src, dst, at):
        own = pltpu.make_async_copy(src(me_t), dst(me_t), own_sem.at[at])
        own.start()

        def start(step, carry):
            k = step // 4
            dy = ring // 2 + jnp.where(lax.rem(k, 2) == 1, -((k + 1) // 2), k // 2)
            peer = at_t(dy, 1 - lax.rem(step // 2, 2), 1 - lax.rem(step, 2))
            send(src, dst, at, "tower", peer, me_t)
            return carry

        lax.fori_loop(0, nt - 1, start, 0)
        return own

    own1 = exchange_i(lambda p: send1.at[p], lambda p: recv1.at[p], 0, groups, True)

    signal(mate_sem, "tower", at_t(0, 0, 1))
    pl.semaphore_wait(mate_sem, 1)
    if ring > 1:
        for step in range(ring // 2):
            signal(over_sem.at[step, 0], "tower", at_t(1, 0, 0))
            signal(over_sem.at[step, 1], "tower", at_t(-1, 0, 0))
            pl.semaphore_wait(over_sem.at[step, 0], 1)
            pl.semaphore_wait(over_sem.at[step, 1], 1)

    s_row = lax.broadcasted_iota(jnp.int32, (samp, samp), 0)
    s_col = lax.broadcasted_iota(jnp.int32, (samp, samp), 1)
    for f in range(feats):
        perm[f] = jnp.where(arr[f : f + 1, :] == s_row, 1.0, 0.0).astype(BF16)
        at = 2 * feats + f
        perm_t[f] = jnp.where(columns[:, at : at + 1] == s_col, 1.0, 0.0).astype(BF16)
    for load in loads[3:]:
        load.wait()

    def all_but_one(ref, sem, count):
        pltpu.make_async_copy(ref.at[pl.ds(0, count - 1)], ref.at[pl.ds(0, count - 1)], sem).wait()

    own1.wait()
    all_but_one(recv1, recv_sem.at[0], ni)

    for f in range(feats):
        got = recv1[:, f].astype(F32).reshape(samp, embed).astype(BF16)
        first[:, f * embed : (f + 1) * embed] = dot(perm[f], got).astype(BF16)

    def forward(layer, src, dst):
        for n in range(tiles):
            cols = slice(n * tile, (n + 1) * tile)
            zval = dot(src[...], cw_ref[layer, :, cols]) + cb_ref[layer : layer + 1, cols]
            zbuf[layer, :, cols] = zval
            dst[:, cols] = (first[:, cols].astype(F32) * zval + src[:, cols].astype(F32)).astype(BF16)

    forward(0, first, state1)
    forward(1, state1, state2)
    csend[...] = dot(state2[...], sq_ref[...]).reshape(nt, samp // nt, -1).astype(BF16)

    own2 = exchange_t(lambda p: csend.at[p], lambda p: joined.at[p], 1)
    own2.wait()
    all_but_one(joined, recv_sem.at[1], nt)

    comp = joined.shape[2]
    whole = jnp.concatenate([joined[t] for t in range(nt)], axis=1)
    pre = dot(whole, ow_ref[...]) + ob_ref[...]
    sig = jax.nn.sigmoid(pre)
    out_ref[0, 0] = (pre * sig).astype(BF16)
    dz = (ct_ref[...].astype(F32) * (sig * (1.0 + pre * (1.0 - sig)))).astype(BF16)
    d_in = dot_t(dz, ow_ref[...]).astype(BF16)
    for t in range(nt):
        dsend[t] = d_in[:, t * comp : (t + 1) * comp]

    own3 = exchange_t(lambda p: dsend.at[p], lambda p: dcomp.at[p], 2)
    own3.wait()
    all_but_one(dcomp, recv_sem.at[2], nt)

    dc = dcomp[...].astype(F32).reshape(samp, comp).astype(BF16)

    def back_top(n):
        cols = slice(n * tile, (n + 1) * tile)
        grad = dot_t(dc, sq_ref[cols, :])
        gbuf[:, cols] = grad
        direct[:, cols] = grad * zbuf[1, :, cols]
        upd[1, :, cols] = (grad * first[:, cols].astype(F32)).astype(BF16)

    def back_one(n):
        cols = slice(n * tile, (n + 1) * tile)
        grad = gbuf[:, cols] + dot_t(upd[1], cw_ref[1, cols, :])
        gbuf[:, cols] = grad
        direct[:, cols] += grad * zbuf[0, :, cols]
        upd[0, :, cols] = (grad * first[:, cols].astype(F32)).astype(BF16)

    def back_zero(n):
        cols = slice(n * tile, (n + 1) * tile)
        grad = gbuf[:, cols] + dot_t(upd[0], cw_ref[0, cols, :])
        final[:, cols] = (grad + direct[:, cols]).astype(BF16)

    for n in range(tiles):
        back_top(n)
    for n in range(tiles):
        back_one(n)
    for n in range(tiles):
        back_zero(n)
    for f in range(feats):
        leaving = dot(perm_t[f], final[:, f * embed : (f + 1) * embed])
        send2[:, f] = leaving.reshape(ni, block, embed).astype(BF16)

    own4 = exchange_i(lambda p: send2.at[p], lambda p: grad_ref.at[:, p], 3, 1, False)
    own4.wait()
    pltpu.make_async_copy(
        grad_ref.at[:, pl.ds(0, ni - 1)], grad_ref.at[:, pl.ds(0, ni - 1)], recv_sem.at[3]
    ).wait()
    all_but_one(send1, send_sem.at[0], ni)
    all_but_one(csend, send_sem.at[1], nt)
    all_but_one(dsend, send_sem.at[2], nt)
    all_but_one(send2, send_sem.at[3], ni)


def local(ids, arrival, tables, cross_weight, cross_bias, squeeze, over_weight, over_bias, cotangent, ni, nt, groups=4, cid=0, name=None, vmem=32):
    feats, rows, embed = tables.shape
    samp = arrival.shape[1]
    width = cross_weight.shape[2]
    comp = squeeze.shape[2]
    wide = over_weight.shape[1]
    rblock = cotangent.shape[2]
    block = samp // ni
    any_spec = pl.BlockSpec(memory_space=pltpu.HBM)
    vmem_spec = pl.BlockSpec(memory_space=pltpu.VMEM)
    over_out, grad = pl.pallas_call(
        functools.partial(kernel, ni, nt, groups),
        out_shape=(
            jax.ShapeDtypeStruct(cotangent.shape, BF16),
            jax.ShapeDtypeStruct((feats, ni, block, embed), BF16),
        ),
        in_specs=[any_spec] * 9,
        name=name,
        out_specs=(vmem_spec, vmem_spec),
        scratch_shapes=[
            pltpu.VMEM((feats, 2, samp), jnp.int32),
            pltpu.VMEM((feats, samp), jnp.int32),
            pltpu.VMEM((feats, rows, embed), BF16),
            pltpu.VMEM((2, width, width), BF16),
            pltpu.VMEM((2, width), F32),
            pltpu.VMEM((width, comp), BF16),
            pltpu.VMEM((nt * comp, wide), BF16),
            pltpu.VMEM((1, wide), F32),
            pltpu.VMEM((rblock, wide), BF16),
            pltpu.VMEM((ni, feats, block, embed), BF16),
            pltpu.VMEM((ni, feats, block, embed), BF16),
            pltpu.VMEM((nt, rblock, comp), BF16),
            pltpu.VMEM((nt, rblock, comp), BF16),
            pltpu.VMEM((nt, rblock, comp), BF16),
            pltpu.VMEM((nt, rblock, comp), BF16),
            pltpu.VMEM((ni, feats, block, embed), BF16),
            pltpu.VMEM((feats, samp, samp), BF16),
            pltpu.VMEM((feats, samp, samp), BF16),
            pltpu.VMEM((samp, width), BF16),
            pltpu.VMEM((samp, width), BF16),
            pltpu.VMEM((samp, width), BF16),
            pltpu.VMEM((2, samp, width), F32),
            pltpu.VMEM((samp, width), F32),
            pltpu.VMEM((samp, width), F32),
            pltpu.VMEM((2, samp, width), BF16),
            pltpu.VMEM((samp, width), BF16),
            pltpu.SemaphoreType.DMA((9,)),
            pltpu.SemaphoreType.DMA((4,)),
            pltpu.SemaphoreType.DMA((4,)),
            pltpu.SemaphoreType.DMA((4,)),
            pltpu.SemaphoreType.REGULAR((ni // 4, 2)),
            pltpu.SemaphoreType.REGULAR((max(1, nt // 8), 2)),
            pltpu.SemaphoreType.REGULAR,
        ],
        compiler_params=pltpu.CompilerParams(
            collective_id=cid, has_side_effects=True, vmem_limit_bytes=vmem * 1024 * 1024
        ),
    )(
        *(
            pltpu.with_memory_space_constraint(x, pltpu.HBM)
            for x in (
                ids,
                arrival,
                tables,
                cross_weight,
                cross_bias,
                squeeze,
                over_weight,
                over_bias[None, :],
                cotangent,
            )
        )
    )
    return over_out, grad.reshape(feats, samp, embed)


def solution(mesh):
    in_specs = (
        P("tower", None, "intra"),
        P("tower", "intra"),
        P("tower", "intra", None),
        P("tower", None, None, None),
        P("tower", None, None),
        P("tower", None, None),
        P(),
        P(),
        P("intra", "tower", None, None),
    )
    out_specs = (P("intra", "tower", None, None), P("tower", "intra", None))
    body = functools.partial(local, ni=mesh.shape["intra"], nt=mesh.shape["tower"])
    return jax.shard_map(body, mesh=mesh, in_specs=in_specs, out_specs=out_specs, check_vma=False)
```

```python
import functools

import jax
import jax.numpy as jnp
from jax import lax
from jax.experimental import pallas as pl
from jax.experimental.pallas import tpu as pltpu
from jax.sharding import PartitionSpec as P

MESH = pl.DeviceIdType.MESH
F32 = jnp.float32
BF16 = jnp.bfloat16
NT_DIMS = (((1,), (1,)), ((), ()))


def dot(a, b):
    return jnp.dot(a, b, preferred_element_type=F32)


def dot_t(a, b):
    return lax.dot_general(a, b, NT_DIMS, preferred_element_type=F32)


def kernel(
    ni,
    nt,
    groups,
    ids_hbm,
    arr_hbm,
    tab_hbm,
    cw_hbm,
    cb_hbm,
    sq_hbm,
    ow_hbm,
    ob_hbm,
    ct_hbm,
    out_ref,
    grad_ref,
    ids_ref,
    arr_ref,
    tab_ref,
    cw_ref,
    cb_ref,
    sq_ref,
    ow_ref,
    ob_ref,
    ct_ref,
    send1,
    recv1,
    csend,
    joined,
    dsend,
    dcomp,
    send2,
    perm,
    perm_t,
    first,
    state1,
    state2,
    zbuf,
    gbuf,
    direct,
    upd,
    final,
    in_sem,
    own_sem,
    send_sem,
    recv_sem,
):
    feats, rows, embed = tab_ref.shape
    samp = arr_ref.shape[1]
    width = cw_ref.shape[2]
    block = samp // ni
    half = ni // 2
    tile = min(256, width)
    tiles = width // tile
    me_i = lax.axis_index("intra")
    me_t = lax.axis_index("tower")

    loads = [
        pltpu.make_async_copy(src, dst, in_sem.at[at])
        for at, (src, dst) in enumerate(
            (
                (ids_hbm, ids_ref),
                (arr_hbm, arr_ref),
                (tab_hbm, tab_ref),
                (cw_hbm.at[0], cw_ref),
                (cb_hbm.at[0], cb_ref),
                (sq_hbm.at[0], sq_ref),
                (ow_hbm, ow_ref),
                (ob_hbm, ob_ref),
                (ct_hbm.at[0, 0], ct_ref),
            )
        )
    ]
    for load in loads[:3]:
        load.start()

    barrier = pltpu.get_barrier_semaphore()

    def peer_of(step, sets):
        each = half // sets
        k = step // 2 % each
        shift = (-((k + 1) // 2) if k % 2 else k // 2) + each // 2
        base = lax.rem((step // 2) // each + half - me_i // 2, sets)
        z = lax.rem(me_i // 2 + base + sets * shift, half)
        xh = lax.rem(lax.rem(me_i, 2) + 1 - step % 2, 2)
        return z * 2 + xh

    def greet_t(step, carry):
        peer = lax.rem(me_t + step, nt)
        pl.semaphore_signal(barrier, inc=1, device_id={"tower": peer}, device_id_type=MESH)
        return carry

    for step in range(ni - 1):
        peer = peer_of(step, 1)
        pl.semaphore_signal(barrier, inc=1, device_id={"intra": peer}, device_id_type=MESH)
    lax.fori_loop(1, nt, greet_t, 0)

    for load in loads[3:]:
        load.start()
    loads[0].wait()
    loads[1].wait()

    ids = ids_ref[...].reshape(feats * 2, samp)
    arr = arr_ref[...]
    pad = jnp.zeros((128 - 3 * feats, samp), jnp.int32)
    columns = jnp.concatenate([ids, arr, pad], axis=0).T

    loads[2].wait()
    row_id = lax.broadcasted_iota(jnp.int32, (samp, rows), 1)
    for f in range(feats):
        hot = jnp.where(columns[:, 2 * f : 2 * f + 1] == row_id, 1.0, 0.0)
        hot = hot + jnp.where(columns[:, 2 * f + 1 : 2 * f + 2] == row_id, 1.0, 0.0)
        pooled = dot(hot.astype(BF16), tab_ref[f])
        send1[:, f] = pooled.reshape(ni, block, embed).astype(BF16)

    pl.semaphore_wait(barrier, ni + nt - 2)

    def exchange_i(src, dst, at, sets):
        own = pltpu.make_async_copy(src(me_i), dst(me_i), own_sem.at[at])
        own.start()

        def start(step):
            peer = peer_of(step, sets)

            @pl.when(peer != me_i)
            def _():
                pltpu.make_async_remote_copy(
                    src_ref=src(peer),
                    dst_ref=dst(me_i),
                    send_sem=send_sem.at[at],
                    recv_sem=recv_sem.at[at],
                    device_id={"intra": peer},
                    device_id_type=MESH,
                ).start()

        for step in range(ni):
            start(step)
        return own

    def exchange_t(src, dst, at):
        own = pltpu.make_async_copy(src(me_t), dst(me_t), own_sem.at[at])
        own.start()

        ring = nt // 4
        low, why, core = me_t // (2 * ring), lax.rem(me_t // 2, ring), lax.rem(me_t, 2)

        def go(peer):
            pltpu.make_async_remote_copy(
                src_ref=src(peer),
                dst_ref=dst(me_t),
                send_sem=send_sem.at[at],
                recv_sem=recv_sem.at[at],
                device_id={"tower": peer},
                device_id_type=MESH,
            ).start()

        def far(step):
            k = step // 4
            dy = ring // 2 + (-((k + 1) // 2) if k % 2 else k // 2)
            flip_low, flip_core = 1 - step // 2 % 2, 1 - step % 2
            return (
                lax.rem(low + flip_low, 2) * (2 * ring) + lax.rem(why + dy, ring) * 2 + lax.rem(core + flip_core, 2)
            )

        for step in range(nt - 1):
            go(far(step))
        return own

    own1 = exchange_i(lambda p: send1.at[p], lambda p: recv1.at[p], 0, groups)

    s_row = lax.broadcasted_iota(jnp.int32, (samp, samp), 0)
    s_col = lax.broadcasted_iota(jnp.int32, (samp, samp), 1)
    for f in range(feats):
        perm[f] = jnp.where(arr[f : f + 1, :] == s_row, 1.0, 0.0).astype(BF16)
        at = 2 * feats + f
        perm_t[f] = jnp.where(columns[:, at : at + 1] == s_col, 1.0, 0.0).astype(BF16)
    for load in loads[3:]:
        load.wait()

    def all_but_one(ref, sem, count):
        pltpu.make_async_copy(ref.at[pl.ds(0, count - 1)], ref.at[pl.ds(0, count - 1)], sem).wait()

    own1.wait()
    all_but_one(recv1, recv_sem.at[0], ni)

    for f in range(feats):
        got = recv1[:, f].astype(F32).reshape(samp, embed).astype(BF16)
        first[:, f * embed : (f + 1) * embed] = dot(perm[f], got).astype(BF16)

    def forward(layer, src, dst):
        for n in range(tiles):
            cols = slice(n * tile, (n + 1) * tile)
            zval = dot(src[...], cw_ref[layer, :, cols]) + cb_ref[layer : layer + 1, cols]
            zbuf[layer, :, cols] = zval
            dst[:, cols] = (first[:, cols].astype(F32) * zval + src[:, cols].astype(F32)).astype(BF16)

    forward(0, first, state1)
    forward(1, state1, state2)
    csend[...] = dot(state2[...], sq_ref[...]).reshape(nt, samp // nt, -1).astype(BF16)

    own2 = exchange_t(lambda p: csend.at[p], lambda p: joined.at[p], 1)
    own2.wait()
    all_but_one(joined, recv_sem.at[1], nt)

    comp = joined.shape[2]
    whole = jnp.concatenate([joined[t] for t in range(nt)], axis=1)
    pre = dot(whole, ow_ref[...]) + ob_ref[...]
    sig = jax.nn.sigmoid(pre)
    out_ref[0, 0] = (pre * sig).astype(BF16)
    dz = (ct_ref[...].astype(F32) * (sig * (1.0 + pre * (1.0 - sig)))).astype(BF16)
    d_in = dot_t(dz, ow_ref[...]).astype(BF16)
    for t in range(nt):
        dsend[t] = d_in[:, t * comp : (t + 1) * comp]

    own3 = exchange_t(lambda p: dsend.at[p], lambda p: dcomp.at[p], 2)
    own3.wait()
    all_but_one(dcomp, recv_sem.at[2], nt)

    dc = dcomp[...].astype(F32).reshape(samp, comp).astype(BF16)

    def back_top(n):
        cols = slice(n * tile, (n + 1) * tile)
        grad = dot_t(dc, sq_ref[cols, :])
        gbuf[:, cols] = grad
        direct[:, cols] = grad * zbuf[1, :, cols]
        upd[1, :, cols] = (grad * first[:, cols].astype(F32)).astype(BF16)

    def back_one(n):
        cols = slice(n * tile, (n + 1) * tile)
        grad = gbuf[:, cols] + dot_t(upd[1], cw_ref[1, cols, :])
        gbuf[:, cols] = grad
        direct[:, cols] += grad * zbuf[0, :, cols]
        upd[0, :, cols] = (grad * first[:, cols].astype(F32)).astype(BF16)

    def back_zero(n):
        cols = slice(n * tile, (n + 1) * tile)
        grad = gbuf[:, cols] + dot_t(upd[0], cw_ref[0, cols, :])
        final[:, cols] = (grad + direct[:, cols]).astype(BF16)

    for n in range(tiles):
        back_top(n)
    for n in range(tiles):
        back_one(n)
    for n in range(tiles):
        back_zero(n)
    for f in range(feats):
        leaving = dot(perm_t[f], final[:, f * embed : (f + 1) * embed])
        send2[:, f] = leaving.reshape(ni, block, embed).astype(BF16)

    own4 = exchange_i(lambda p: send2.at[p], lambda p: grad_ref.at[:, p], 3, 1)
    own4.wait()
    pltpu.make_async_copy(
        grad_ref.at[:, pl.ds(0, ni - 1)], grad_ref.at[:, pl.ds(0, ni - 1)], recv_sem.at[3]
    ).wait()
    all_but_one(send1, send_sem.at[0], ni)
    all_but_one(csend, send_sem.at[1], nt)
    all_but_one(dsend, send_sem.at[2], nt)
    all_but_one(send2, send_sem.at[3], ni)


def local(ids, arrival, tables, cross_weight, cross_bias, squeeze, over_weight, over_bias, cotangent, ni, nt, groups=4, cid=0, name=None, vmem=32):
    feats, rows, embed = tables.shape
    samp = arrival.shape[1]
    width = cross_weight.shape[2]
    comp = squeeze.shape[2]
    wide = over_weight.shape[1]
    rblock = cotangent.shape[2]
    block = samp // ni
    any_spec = pl.BlockSpec(memory_space=pltpu.HBM)
    vmem_spec = pl.BlockSpec(memory_space=pltpu.VMEM)
    over_out, grad = pl.pallas_call(
        functools.partial(kernel, ni, nt, groups),
        out_shape=(
            jax.ShapeDtypeStruct(cotangent.shape, BF16),
            jax.ShapeDtypeStruct((feats, ni, block, embed), BF16),
        ),
        in_specs=[any_spec] * 9,
        name=name,
        out_specs=(vmem_spec, vmem_spec),
        scratch_shapes=[
            pltpu.VMEM((feats, 2, samp), jnp.int32),
            pltpu.VMEM((feats, samp), jnp.int32),
            pltpu.VMEM((feats, rows, embed), BF16),
            pltpu.VMEM((2, width, width), BF16),
            pltpu.VMEM((2, width), F32),
            pltpu.VMEM((width, comp), BF16),
            pltpu.VMEM((nt * comp, wide), BF16),
            pltpu.VMEM((1, wide), F32),
            pltpu.VMEM((rblock, wide), BF16),
            pltpu.VMEM((ni, feats, block, embed), BF16),
            pltpu.VMEM((ni, feats, block, embed), BF16),
            pltpu.VMEM((nt, rblock, comp), BF16),
            pltpu.VMEM((nt, rblock, comp), BF16),
            pltpu.VMEM((nt, rblock, comp), BF16),
            pltpu.VMEM((nt, rblock, comp), BF16),
            pltpu.VMEM((ni, feats, block, embed), BF16),
            pltpu.VMEM((feats, samp, samp), BF16),
            pltpu.VMEM((feats, samp, samp), BF16),
            pltpu.VMEM((samp, width), BF16),
            pltpu.VMEM((samp, width), BF16),
            pltpu.VMEM((samp, width), BF16),
            pltpu.VMEM((2, samp, width), F32),
            pltpu.VMEM((samp, width), F32),
            pltpu.VMEM((samp, width), F32),
            pltpu.VMEM((2, samp, width), BF16),
            pltpu.VMEM((samp, width), BF16),
            pltpu.SemaphoreType.DMA((9,)),
            pltpu.SemaphoreType.DMA((4,)),
            pltpu.SemaphoreType.DMA((4,)),
            pltpu.SemaphoreType.DMA((4,)),
        ],
        compiler_params=pltpu.CompilerParams(
            collective_id=cid, has_side_effects=True, vmem_limit_bytes=vmem * 1024 * 1024
        ),
    )(
        *(
            pltpu.with_memory_space_constraint(x, pltpu.HBM)
            for x in (
                ids,
                arrival,
                tables,
                cross_weight,
                cross_bias,
                squeeze,
                over_weight,
                over_bias[None, :],
                cotangent,
            )
        )
    )
    return over_out, grad.reshape(feats, samp, embed)


def solution(mesh):
    in_specs = (
        P("tower", None, "intra"),
        P("tower", "intra"),
        P("tower", "intra", None),
        P("tower", None, None, None),
        P("tower", None, None),
        P("tower", None, None),
        P(),
        P(),
        P("intra", "tower", None, None),
    )
    out_specs = (P("intra", "tower", None, None), P("tower", "intra", None))
    body = functools.partial(local, ni=mesh.shape["intra"], nt=mesh.shape["tower"])
    return jax.shard_map(body, mesh=mesh, in_specs=in_specs, out_specs=out_specs, check_vma=False)
```
